32 devices in a mesh: ep: 8 (over z, y), tp: 4 (over x, core).
Axes of the slice: x: 2, y: 2, z: 4, core: 2. Of those that a mesh axis runs over, the one named last changes fastest.
Arguments:
- tokens: bfloat16 [1024, 4096], P('ep', 'tp'), may hold values from -6 to 6
- out_grad: bfloat16 [1024, 4096], P('ep', 'tp'), may hold values from -6 to 6
- expert_ids: int32 [1024, 4], P('ep'), may hold values from 0 to 7, all different within a row; in each aligned block of 128 rows (0 to 127, 128 to 255, ...) at most 72 rows name the same one
- route_probs: float32 [1024, 4], P('ep'), may hold values from 0.05 to 0.5
- w_gate: bfloat16 [8, 4096, 768], P('ep', 'tp'), may hold values from -0.09375 to 0.09375
- w_up: bfloat16 [8, 4096, 768], P('ep', 'tp'), may hold values from -0.09375 to 0.09375
- w_down: bfloat16 [8, 768, 4096], P('ep', None, 'tp'), may hold values from -0.21875 to 0.21875
Outputs:
- grad_tokens: bfloat16 [1024, 4096], P('ep', 'tp')
- fisher_gate: bfloat16 [8, 4096, 768], P('ep', 'tp')
- fisher_up: bfloat16 [8, 4096, 768], P('ep', 'tp')
- fisher_down: bfloat16 [8, 768, 4096], P('ep', None, 'tp')
The draws below stay inside these ranges and needn't reach their ends.
Inputs may be any that keep to these rules, and one draw needn't show every extreme that they name: `expert_ids`: each token names 4 different experts; among the tokens of one index of ep no expert is named by more than 72 tokens, a bound that some block reaches.
All inputs are finite; a program needn't handle non-finite values.
Results may differ from the reference program's by a relative error of at most 0.03.
Values may be sent and summed in bfloat16 or wider, within the bound.
A program may use at most 128 MiB of HBM per device.

```python
import math
import jax
import jax.numpy as jnp
import numpy as np
from jax import lax

D = 4096
FF = 768
TOK_DEV = 128
TOKENS = 1024
EXPERTS = 8
TOPK = 4
CAP = 72
N_EP = 8
N_TP = 4


def block_levels(stream_key, extent, shards, low, high):
    loudness, own = 1.0, jax.random.fold_in(stream_key, 6)
    for axis_at, blocks in shards:
        draws = jnp.exp(jax.random.uniform(jax.random.fold_in(own, axis_at), (blocks,), jnp.float32, low / len(shards), high / len(shards)))
        loudness = loudness * jnp.repeat(draws, extent[axis_at] // blocks).reshape([-1 if axis == axis_at else 1 for axis in range(len(extent))])
    return loudness


def routed_block(rng, own, number, rows, count, top, bound, skew):
    order = jax.random.permutation(rng, count)
    packed, common = load_shares(count, rows * top, bound, skew, True), load_shares(count, rows * top, bound, skew, False)
    places = jnp.arange(count)

    def named(lengths, rotation):
        used = int((lengths > 0).sum())
        fixed = max(1, used // 4)
        moved = fixed + (places - fixed + rotation * (used - fixed)) % max(1, count - fixed)
        return jnp.zeros((count,), jnp.int32).at[order[jnp.where(places < fixed, places, moved)]].set(jnp.asarray(lengths, jnp.int32))

    lengths = jnp.where(number % 4 == 0, named(packed, number // 4), named(common, number - number // 4 - 1))
    mixed = jax.random.permutation(jax.random.fold_in(own, 3), count)
    giver, sink = mixed[0:count // 2 * 2:2], mixed[1:count // 2 * 2:2]
    room = jnp.minimum(lengths[giver] - 1, bound - lengths[sink]) // 2
    room = jnp.where((giver == order[0]) | (sink == order[0]) | (lengths[sink] == 0), 0, jnp.maximum(room, 0))
    moved = jax.random.randint(jax.random.fold_in(own, 4), (count // 2,), 0, 1 << 20) % (room + 1)
    lengths = lengths.at[giver].add(-moved).at[sink].add(moved)
    labels = jnp.searchsorted(jnp.cumsum(lengths), jnp.arange(rows * top), side="right").astype(jnp.int32)
    grid = labels.reshape(top, rows).T
    grid = grid[jax.random.permutation(jax.random.fold_in(own, 1), rows)]
    rotation = jax.random.randint(jax.random.fold_in(own, 2), (rows, 1), 0, top)
    return jnp.take_along_axis(grid, (jnp.arange(top)[None, :] + rotation) % top, axis=1)


def load_shares(number_of, total, reach, slope, full):
    loads = [(1 << 20) // math.isqrt(standing ** slope) + 1 for standing in range(1, number_of + 1)]
    largest = reach if full else min(reach, max(-(-total // number_of), total * loads[0] // sum(loads)))
    least = 1 if total - largest >= number_of - 1 else 0
    given, surplus = [largest] + [least] * (number_of - 1), total - largest - least * (number_of - 1)
    while surplus > 0:
        free = [i for i in range(1, number_of) if given[i] < largest] or [i for i in range(1, number_of) if given[i] < reach]
        whole, left = sum([loads[i] for i in free]), surplus
        for i in free:
            more = min(reach - given[i], max(1, left * loads[i] // whole), surplus)
            given[i] = given[i] + more
            surplus = surplus - more
    return np.array(given)


def normal_values(key, extent, scale, bound, cuts=(), held_as=jnp.bfloat16):
    values = jax.random.normal(key, extent, jnp.float32) * scale
    if len(cuts) > 0:
        values = block_levels(key, extent, cuts, -0.22, 0.18) * values
    return jnp.clip(values, min=-bound, max=bound).astype(held_as)


def setup_inputs(seed: int = 0) -> dict:
    key_list = jax.random.split(jax.random.key(seed), 8)
    tokens = normal_values(key_list[0], (TOKENS, D), 1.0, 6.0, ((0, 8), (1, 4)))
    out_grad = normal_values(key_list[1], (TOKENS, D), 1.0, 6.0, ((0, 8), (1, 4)))
    expert_ids_keys = jax.random.split(jax.random.fold_in(key_list[2], 1), TOKENS // TOK_DEV)
    expert_ids_turns = jax.random.permutation(jax.random.fold_in(key_list[2], 3), TOKENS // TOK_DEV)
    expert_ids = jax.vmap(lambda own, number: routed_block(jax.random.fold_in(key_list[2], 2), own, number, TOK_DEV, EXPERTS, TOPK, CAP, 2))(expert_ids_keys, expert_ids_turns).reshape((TOKENS, TOPK))
    route_probs = jnp.clip(jnp.exp(math.log(0.5) - 2.3025851 * jax.random.uniform(key_list[3], (TOKENS, TOPK), jnp.float32) ** block_levels(key_list[3], (TOKENS, TOPK), ((0, 8),), -0.2, 0.2)), 0.05, 0.5)
    w_gate = normal_values(key_list[4], (EXPERTS, D, FF), D ** -0.5, 0.09375, ((0, 8), (1, 4)))
    w_up = normal_values(key_list[5], (EXPERTS, D, FF), D ** -0.5, 0.09375, ((0, 8), (1, 4)))
    w_down = normal_values(key_list[6], (EXPERTS, FF, D), FF ** -0.5, 0.21875, ((0, 8), (2, 4)))
    return dict(tokens=tokens, out_grad=out_grad, expert_ids=expert_ids, route_probs=route_probs, w_gate=w_gate, w_up=w_up, w_down=w_down)


def reference(tokens, out_grad, expert_ids, route_probs, w_gate, w_up, w_down):
    assigns = TOK_DEV * TOPK
    quarter = D // N_TP
    blocks = expert_ids.reshape(N_EP, assigns).astype(jnp.int32)
    onehot = (blocks[:, :, None] == jnp.arange(EXPERTS, dtype=jnp.int32)[None, None, :]).astype(jnp.int32)
    ranks = jnp.sum((jnp.cumsum(onehot, 1) - onehot) * onehot, 2).astype(jnp.int32)
    slots = (blocks * CAP + ranks).astype(jnp.int32)
    global_ids = (jnp.arange(N_EP, dtype=jnp.int32) * assigns)[:, None] + jnp.arange(assigns, dtype=jnp.int32)[None, :]

    def fill_row(slot_row, id_row):
        return jnp.full((EXPERTS * CAP,), TOKENS * TOPK, jnp.int32).at[slot_row].set(id_row)

    table = jax.vmap(fill_row)(slots, global_ids)
    table = table.reshape(N_EP, EXPERTS, CAP).transpose(1, 0, 2).reshape(EXPERTS, N_EP * CAP)
    padded_x = jnp.concatenate([tokens, jnp.zeros((1, D), tokens.dtype)], 0)
    padded_dy = jnp.concatenate([out_grad, jnp.zeros((1, D), out_grad.dtype)], 0)
    padded_p = jnp.concatenate([route_probs.reshape(-1), jnp.zeros((1,), jnp.float32)], 0)
    scale = 1.0 / TOK_DEV

    def expert_step(accum, inputs):
        e_table, gate_mat, up_mat, down_mat = inputs
        token_of = (e_table // TOPK).astype(jnp.int32)
        x_rows = padded_x[token_of]
        dy_rows = (padded_dy[token_of].astype(jnp.float32) * padded_p[e_table][:, None]).astype(jnp.bfloat16)
        x_quart = x_rows.astype(jnp.float32).reshape(-1, N_TP, quarter)
        dy_quart = dy_rows.astype(jnp.float32).reshape(-1, N_TP, quarter)
        gate = jnp.sum(jnp.einsum('sqd,qdf->qsf', x_quart, gate_mat.astype(jnp.float32).reshape(N_TP, quarter, FF)).astype(jnp.bfloat16).astype(jnp.float32), 0)
        up = jnp.sum(jnp.einsum('sqd,qdf->qsf', x_quart, up_mat.astype(jnp.float32).reshape(N_TP, quarter, FF)).astype(jnp.bfloat16).astype(jnp.float32), 0)
        dact = jnp.sum(jnp.einsum('sqd,fqd->qsf', dy_quart, down_mat.astype(jnp.float32).reshape(FF, N_TP, quarter)).astype(jnp.bfloat16).astype(jnp.float32), 0)
        sig = jax.nn.sigmoid(gate)
        act = (gate * sig * up).astype(jnp.bfloat16)
        dgate = (dact * up * sig * (1.0 + gate * (1.0 - sig))).astype(jnp.bfloat16)
        dup = (dact * gate * sig).astype(jnp.bfloat16)
        dx_rows = (jnp.dot(dgate, gate_mat.T, preferred_element_type=jnp.float32) + jnp.dot(dup, up_mat.T, preferred_element_type=jnp.float32)).astype(jnp.bfloat16)
        accum = accum.at[token_of].add(dx_rows.astype(jnp.float32))
        x_sq = jnp.square(x_rows.astype(jnp.float32)).astype(jnp.bfloat16)
        act_sq = jnp.square(act.astype(jnp.float32)).astype(jnp.bfloat16)
        dg_sq = jnp.square(dgate.astype(jnp.float32)).astype(jnp.bfloat16)
        du_sq = jnp.square(dup.astype(jnp.float32)).astype(jnp.bfloat16)
        dy_sq = jnp.square(dy_rows.astype(jnp.float32)).astype(jnp.bfloat16)
        fish_gate = (jnp.dot(x_sq.T, dg_sq, preferred_element_type=jnp.float32) * scale).astype(jnp.bfloat16)
        fish_up = (jnp.dot(x_sq.T, du_sq, preferred_element_type=jnp.float32) * scale).astype(jnp.bfloat16)
        fish_down = (jnp.dot(act_sq.T, dy_sq, preferred_element_type=jnp.float32) * scale).astype(jnp.bfloat16)
        return accum, (fish_gate, fish_up, fish_down)

    start = jnp.zeros((TOKENS + 1, D), jnp.float32)
    accum, outs = lax.scan(expert_step, start, (table, w_gate, w_up, w_down))
    grad_tokens = accum[:TOKENS].astype(jnp.bfloat16)
    return grad_tokens, outs[0], outs[1], outs[2]
```

```python
import functools

import jax
import jax.numpy as jnp
from jax import lax
from jax.experimental import pallas as pl
from jax.experimental.pallas import tpu as pltpu
from jax.sharding import PartitionSpec as P


def contract_rows(left, right):
    return lax.dot_general(
        left, right, (((0,), (0,)), ((), ())), preferred_element_type=jnp.float32
    )


def contract_cols(left, right):
    return lax.dot_general(
        left, right, (((1,), (1,)), ((), ())), preferred_element_type=jnp.float32
    )


def swiglu_back(gate, up, dact):
    sig = jax.nn.sigmoid(gate)
    act = (gate * sig * up).astype(jnp.bfloat16)
    dgate = (dact * up * sig * (1.0 + gate * (1.0 - sig))).astype(jnp.bfloat16)
    dup = (dact * gate * sig).astype(jnp.bfloat16)
    return (act, dgate, dup)


def squared(values):
    return jnp.square(values.astype(jnp.float32)).astype(jnp.bfloat16)


def on_device(tokens, out_grad, expert_ids, route_probs, w_gate, w_up, w_down):
    tok_rows = tokens.shape[0]
    width_part = tokens.shape[1]
    top_count = expert_ids.shape[1]
    experts = lax.axis_size("ep")
    capacity = tok_rows * top_count * 9 // (8 * experts)
    assigns = tok_rows * top_count
    flat_ids = expert_ids.reshape(-1)
    onehot = (flat_ids[:, None] == jnp.arange(experts, dtype=jnp.int32)[None, :]).astype(jnp.int32)
    ranks = jnp.sum((jnp.cumsum(onehot, 0) - onehot) * onehot, 1)
    slot_index = flat_ids * capacity + ranks
    table = (
        jnp.full((experts * capacity,), assigns, jnp.int32)
        .at[slot_index]
        .set(jnp.arange(assigns, dtype=jnp.int32))
    )
    token_of = table // top_count
    padded_x = jnp.concatenate([tokens, jnp.zeros((1, width_part), tokens.dtype)], 0)
    padded_dy = jnp.concatenate([out_grad, jnp.zeros((1, width_part), out_grad.dtype)], 0)
    padded_p = jnp.concatenate([route_probs.reshape(-1), jnp.zeros((1,), jnp.float32)], 0)
    send_x = padded_x[token_of].reshape(experts, capacity, width_part)
    send_dy = (padded_dy[token_of].astype(jnp.float32) * padded_p[table][:, None]).astype(
        jnp.bfloat16
    )
    send_dy = send_dy.reshape(experts, capacity, width_part)
    gate_mat = w_gate[0]
    up_mat = w_up[0]
    down_mat = w_down[0]
    recv_x, recv_dy = (
        lax.all_to_all(send_x, "ep", split_axis=0, concat_axis=0, tiled=True),
        lax.all_to_all(send_dy, "ep", split_axis=0, concat_axis=0, tiled=True),
    )
    recv_x = recv_x.reshape(-1, width_part)
    recv_dy = recv_dy.reshape(-1, width_part)
    gate_part = jnp.dot(recv_x, gate_mat, preferred_element_type=jnp.float32)
    up_part = jnp.dot(recv_x, up_mat, preferred_element_type=jnp.float32)
    dact_part = contract_cols(recv_dy, down_mat)
    gate, up, dact = (
        lax.psum(gate_part.astype(jnp.bfloat16), "tp").astype(jnp.float32),
        lax.psum(up_part.astype(jnp.bfloat16), "tp").astype(jnp.float32),
        lax.psum(dact_part.astype(jnp.bfloat16), "tp").astype(jnp.float32),
    )
    act, dgate, dup = swiglu_back(gate, up, dact)
    dx_rows = (contract_cols(dgate, gate_mat) + contract_cols(dup, up_mat)).astype(jnp.bfloat16)
    returned = lax.all_to_all(
        dx_rows.reshape(experts, capacity, width_part),
        "ep",
        split_axis=0,
        concat_axis=0,
        tiled=True,
    )
    scale = 1.0 / tok_rows
    x_sq = squared(recv_x)
    fisher_gate = (contract_rows(x_sq, squared(dgate)) * scale).astype(jnp.bfloat16)[None]
    fisher_up = (contract_rows(x_sq, squared(dup)) * scale).astype(jnp.bfloat16)[None]
    fisher_down = (contract_rows(squared(act), squared(recv_dy)) * scale).astype(jnp.bfloat16)[None]
    pulled = returned.reshape(experts * capacity, width_part)[slot_index].astype(jnp.float32)
    grad_tokens = jnp.sum(pulled.reshape(tok_rows, top_count, width_part), 1).astype(jnp.bfloat16)
    return (grad_tokens, fisher_gate, fisher_up, fisher_down)


MESH = pl.DeviceIdType.MESH
F32 = jnp.float32
BF16 = jnp.bfloat16
ROW_TILE = 16
LANES = 128
VMEM_BYTES = 60 * 1024 * 1024


def flipped(index, mask):
    out, bit = index, 1
    while bit <= mask:
        if mask & bit:
            out = out + bit * (1 - 2 * ((index // bit) % 2))
        bit *= 2
    return out


def slot_rows(tok_rows, top_count, experts):
    capacity = tok_rows * top_count * 9 // (8 * experts)
    return -(-capacity // ROW_TILE) * ROW_TILE


def fused_kernel(
    n_ep, n_tp, rows,
    tok_ref, og_ref, pe_ref, wg_hbm, wu_hbm, wd_hbm,
    grad_ref, fg_hbm, fu_hbm, fd_hbm,
    wg, wu, wd, rank, onehot, sx, rx, pb, rb, af, dxs, ret, tsq, sqb, fg, fu, fd,
    w_sem, o_sem, xs_sem, xr_sem, ps_sem, pr_sem, as_sem, ar_sem, ds_sem, dr_sem,
):
    e = lax.axis_index("ep")
    q = lax.axis_index("tp")
    tok_rows, width = tok_ref.shape
    ff = wg.shape[1]
    half = ff // 2
    pair = 2 * rows
    chunks = n_ep // 2
    scale = 1.0 / tok_rows

    loads = [
        pltpu.make_async_copy(hbm.at[0], vmem, w_sem.at[i])
        for i, (hbm, vmem) in enumerate(((wg_hbm, wg), (wu_hbm, wu), (wd_hbm, wd)))
    ]
    for copy in loads:
        copy.start()

    barrier = pltpu.get_barrier_semaphore()
    for k in range(1, n_ep):
        pl.semaphore_signal(barrier, inc=1, device_id=(flipped(e, k), q), device_id_type=MESH)
    for j in range(1, n_tp):
        pl.semaphore_signal(barrier, inc=1, device_id=(e, flipped(q, j)), device_id_type=MESH)

    mask = (pe_ref[...] > 0.0).astype(F32)
    before = (
        lax.broadcasted_iota(jnp.int32, (tok_rows, tok_rows), 0)
        < lax.broadcasted_iota(jnp.int32, (tok_rows, tok_rows), 1)
    ).astype(BF16)
    ranks = jnp.dot(mask.astype(BF16), before, preferred_element_type=F32)
    rank[...] = jnp.where(mask > 0.0, ranks, -1.0).astype(jnp.int32)
    slot_iota = lax.broadcasted_iota(jnp.int32, (rows, tok_rows), 0)
    pl.semaphore_wait(barrier, n_ep + n_tp - 2)

    def block(k):
        return pl.ds(k * rows, rows)

    x_copies = [None] * n_ep
    for k in list(range(1, n_ep)) + [0]:
        dest = flipped(e, k)
        hot = (slot_iota == rank[pl.ds(dest, 1), :]).astype(F32)
        hot16 = hot.astype(BF16)
        onehot[block(k), :] = hot16
        xs = jnp.dot(hot16, tok_ref[...], preferred_element_type=F32).astype(BF16)
        prob = jnp.sum(hot * pe_ref[pl.ds(dest, 1), :], 1, keepdims=True)
        dys = (jnp.dot(hot16, og_ref[...], preferred_element_type=F32) * prob).astype(BF16)
        out = rx if k == 0 else sx
        out[0, block(k), :] = xs
        out[1, block(k), :] = dys
        if k:
            copies = []
            for i in range(2):
                copy = pltpu.make_async_remote_copy(
                    src_ref=sx.at[i, block(k), :],
                    dst_ref=rx.at[i, block(k), :],
                    send_sem=xs_sem.at[i, k],
                    recv_sem=xr_sem.at[i, k],
                    device_id=(dest, q),
                    device_id_type=MESH,
                )
                copy.start()
                copies.append(copy)
            x_copies[k] = copies

    def piece(index):
        return (
            pl.ds(pl.multiple_of((index // 2) * rows, ROW_TILE), rows),
            pl.ds(pl.multiple_of((index % 2) * half, LANES), half),
        )

    p_copies = [None] * chunks
    a_copies = [None] * chunks
    d_copies = [None] * n_ep

    def partials(c):
        span = pl.ds(c * pair, pair)
        for k in (2 * c, 2 * c + 1):
            if k:
                x_copies[k][0].wait_recv()
        if c == 0:
            loads[0].wait()
            loads[1].wait()
        x = rx[0, span, :]
        pb[c, 0] = jnp.dot(x, wg[...], preferred_element_type=F32).astype(BF16)
        pb[c, 1] = jnp.dot(x, wu[...], preferred_element_type=F32).astype(BF16)
        for k in (2 * c, 2 * c + 1):
            if k:
                x_copies[k][1].wait_recv()
        if c == 0:
            loads[2].wait()
        pb[c, 2] = contract_cols(rx[1, span, :], wd[...]).astype(BF16)
        p_copies[c] = []
        for j in range(1, n_tp):
            other = flipped(q, j)
            r, l = piece(other)
            copy = pltpu.make_async_remote_copy(
                src_ref=pb.at[c, :, r, l],
                dst_ref=rb.at[c, j - 1],
                send_sem=ps_sem.at[c, j],
                recv_sem=pr_sem.at[c, j],
                device_id=(e, other),
                device_id_type=MESH,
            )
            copy.start()
            p_copies[c].append(copy)

    def activate(c):
        for copy in p_copies[c]:
            copy.wait_recv()
        r, l = piece(q)
        gate, up, dact = [
            pb[c, i, r, l].astype(F32)
            + rb[c, 0, i].astype(F32)
            + rb[c, 1, i].astype(F32)
            + rb[c, 2, i].astype(F32)
            for i in range(3)
        ]
        r = pl.ds(pl.multiple_of(c * pair + (q // 2) * rows, ROW_TILE), rows)
        for i, value in enumerate(swiglu_back(gate, up, dact)):
            af[i, r, l] = value
        a_copies[c] = []
        for j in range(1, n_tp):
            copy = pltpu.make_async_remote_copy(
                src_ref=af.at[:, r, l],
                dst_ref=af.at[:, r, l],
                send_sem=as_sem.at[c, j],
                recv_sem=ar_sem.at[c, j],
                device_id=(e, flipped(q, j)),
                device_id_type=MESH,
            )
            copy.start()
            a_copies[c].append(copy)

    def input_grad(c):
        for j, copy in enumerate(a_copies[c]):
            r, l = piece(flipped(q, j + 1))
            r = pl.ds(
                pl.multiple_of(c * pair + (flipped(q, j + 1) // 2) * rows, ROW_TILE), rows
            )
            pltpu.make_async_remote_copy(
                src_ref=af.at[:, r, l],
                dst_ref=af.at[:, r, l],
                send_sem=as_sem.at[c, j + 1],
                recv_sem=ar_sem.at[c, j + 1],
                device_id=(e, flipped(q, j + 1)),
                device_id_type=MESH,
            ).wait_recv()
        span = pl.ds(c * pair, pair)
        dx = contract_cols(af[1, span, :], wg[...]) + contract_cols(af[2, span, :], wu[...])
        dxs[span, :] = dx.astype(BF16)
        for k in (2 * c, 2 * c + 1):
            if k:
                copy = pltpu.make_async_remote_copy(
                    src_ref=dxs.at[block(k), :],
                    dst_ref=ret.at[block(k), :],
                    send_sem=ds_sem.at[k],
                    recv_sem=dr_sem.at[k],
                    device_id=(flipped(e, k), q),
                    device_id_type=MESH,
                )
                copy.start()
                d_copies[k] = copy
            else:
                ret[block(0), :] = dxs[block(0), :]

    for c in range(chunks + 2):
        if c < chunks:
            partials(c)
        if 0 < c <= chunks:
            activate(c - 1)
        if c > 1:
            input_grad(c - 2)
    def transposed_squares(source, i, columns):
        @pl.loop(0, columns // LANES)
        def _(step):
            l = pl.ds(pl.multiple_of(step * LANES, LANES), LANES)
            tsq[l, :] = squared(source[i, :, l]).T

    def fisher(columns, depth, out):
        @pl.loop(0, columns // LANES)
        def _(step):
            r = pl.ds(pl.multiple_of(step * LANES, LANES), LANES)
            sums = jnp.dot(tsq[r, :], sqb[:, :depth], preferred_element_type=F32)
            out[r, :] = (sums * scale).astype(BF16)

    stores = []

    def store(i, vmem, hbm):
        copy = pltpu.make_async_copy(vmem, hbm.at[0], o_sem.at[i])
        copy.start()
        stores.append(copy)

    transposed_squares(rx, 0, width)
    sqb[:, :ff] = squared(af[1])
    fisher(width, ff, fg)
    store(0, fg, fg_hbm)
    sqb[:, :ff] = squared(af[2])
    fisher(width, ff, fu)
    store(1, fu, fu_hbm)
    transposed_squares(af, 0, ff)
    sqb[...] = squared(rx[1])
    fisher(ff, width, fd)
    store(2, fd, fd_hbm)

    for k in range(1, n_ep):
        d_copies[k].wait_recv()
    grad_ref[...] = contract_rows(onehot[...], ret[...]).astype(BF16)

    for k in range(1, n_ep):
        for copy in x_copies[k]:
            copy.wait_send()
        d_copies[k].wait_send()
    for c in range(chunks):
        for copy in p_copies[c] + a_copies[c]:
            copy.wait_send()
    for copy in stores:
        copy.wait()


def fused_on_device(n_ep, n_tp, tokens, out_grad, expert_ids, route_probs, w_gate, w_up, w_down):
    tok_rows, width = tokens.shape
    ff = w_gate.shape[2]
    rows = slot_rows(tok_rows, expert_ids.shape[1], n_ep)
    total, chunks = n_ep * rows, n_ep // 2
    names = jnp.arange(n_ep, dtype=jnp.int32)[:, None, None]
    probs = jnp.sum(jnp.where(expert_ids[None] == names, route_probs[None], 0.0), 2)
    any_spec = pl.BlockSpec(memory_space=pl.ANY)
    vmem_spec = pl.BlockSpec(memory_space=pltpu.VMEM)
    dma = pltpu.SemaphoreType.DMA
    return pl.pallas_call(
        functools.partial(fused_kernel, n_ep, n_tp, rows),
        out_shape=(
            jax.ShapeDtypeStruct(tokens.shape, BF16),
            jax.ShapeDtypeStruct(w_gate.shape, BF16),
            jax.ShapeDtypeStruct(w_up.shape, BF16),
            jax.ShapeDtypeStruct(w_down.shape, BF16),
        ),
        in_specs=[vmem_spec] * 3 + [any_spec] * 3,
        out_specs=[vmem_spec] + [any_spec] * 3,
        scratch_shapes=[
            pltpu.VMEM((width, ff), BF16),
            pltpu.VMEM((width, ff), BF16),
            pltpu.VMEM((ff, width), BF16),
            pltpu.VMEM((n_ep, tok_rows), jnp.int32),
            pltpu.VMEM((total, tok_rows), BF16),
            pltpu.VMEM((2, total, width), BF16),
            pltpu.VMEM((2, total, width), BF16),
            pltpu.VMEM((chunks, 3, 2 * rows, ff), BF16),
            pltpu.VMEM((chunks, n_tp - 1, 3, rows, ff // 2), BF16),
            pltpu.VMEM((3, total, ff), BF16),
            pltpu.VMEM((total, width), BF16),
            pltpu.VMEM((total, width), BF16),
            pltpu.VMEM((width, total), BF16),
            pltpu.VMEM((total, width), BF16),
            pltpu.VMEM((width, ff), BF16),
            pltpu.VMEM((width, ff), BF16),
            pltpu.VMEM((ff, width), BF16),
            dma((3,)),
            dma((3,)),
            dma((2, n_ep)),
            dma((2, n_ep)),
            dma((chunks, n_tp)),
            dma((chunks, n_tp)),
            dma((chunks, n_tp)),
            dma((chunks, n_tp)),
            dma((n_ep,)),
            dma((n_ep,)),
        ],
        compiler_params=pltpu.CompilerParams(
            collective_id=0, has_side_effects=True, vmem_limit_bytes=VMEM_BYTES
        ),
    )(tokens, out_grad, probs, w_gate, w_up, w_down)


def part(n_ep, n_tp, *args):
    tokens, expert_ids, w_gate = args[0], args[2], args[4]
    width, ff = w_gate.shape[1:]
    rows = slot_rows(tokens.shape[0], expert_ids.shape[1], n_ep)
    fits = (
        n_tp == 4
        and n_ep in (2, 4, 8)
        and ff <= width
        and ff % (2 * LANES) == 0
        and width % LANES == 0
        and n_ep * rows * (17 * width + 18 * ff) + 14 * width * ff < VMEM_BYTES
    )
    if fits:
        return fused_on_device(n_ep, n_tp, *args)
    return on_device(*args)


def solution(mesh):
    in_specs = (
        P("ep", "tp"),
        P("ep", "tp"),
        P("ep", None),
        P("ep", None),
        P("ep", "tp", None),
        P("ep", "tp", None),
        P("ep", None, "tp"),
    )
    out_specs = (P("ep", "tp"), P("ep", "tp", None), P("ep", "tp", None), P("ep", None, "tp"))
    return jax.shard_map(
        functools.partial(part, mesh.shape["ep"], mesh.shape["tp"]), mesh=mesh, in_specs=in_specs, out_specs=out_specs, check_vma=False
    )
```

```python
import functools

import jax
import jax.numpy as jnp
from jax import lax
from jax.experimental import pallas as pl
from jax.experimental.pallas import tpu as pltpu
from jax.sharding import PartitionSpec as P


def contract_rows(left, right):
    return lax.dot_general(
        left, right, (((0,), (0,)), ((), ())), preferred_element_type=jnp.float32
    )


def contract_cols(left, right):
    return lax.dot_general(
        left, right, (((1,), (1,)), ((), ())), preferred_element_type=jnp.float32
    )


def swiglu_back(gate, up, dact):
    sig = jax.nn.sigmoid(gate)
    act = (gate * sig * up).astype(jnp.bfloat16)
    dgate = (dact * up * sig * (1.0 + gate * (1.0 - sig))).astype(jnp.bfloat16)
    dup = (dact * gate * sig).astype(jnp.bfloat16)
    return (act, dgate, dup)


def squared(values):
    return jnp.square(values.astype(jnp.float32)).astype(jnp.bfloat16)


def on_device(tokens, out_grad, expert_ids, route_probs, w_gate, w_up, w_down):
    tok_rows = tokens.shape[0]
    width_part = tokens.shape[1]
    top_count = expert_ids.shape[1]
    experts = lax.axis_size("ep")
    capacity = tok_rows * top_count * 9 // (8 * experts)
    assigns = tok_rows * top_count
    flat_ids = expert_ids.reshape(-1)
    onehot = (flat_ids[:, None] == jnp.arange(experts, dtype=jnp.int32)[None, :]).astype(jnp.int32)
    ranks = jnp.sum((jnp.cumsum(onehot, 0) - onehot) * onehot, 1)
    slot_index = flat_ids * capacity + ranks
    table = (
        jnp.full((experts * capacity,), assigns, jnp.int32)
        .at[slot_index]
        .set(jnp.arange(assigns, dtype=jnp.int32))
    )
    token_of = table // top_count
    padded_x = jnp.concatenate([tokens, jnp.zeros((1, width_part), tokens.dtype)], 0)
    padded_dy = jnp.concatenate([out_grad, jnp.zeros((1, width_part), out_grad.dtype)], 0)
    padded_p = jnp.concatenate([route_probs.reshape(-1), jnp.zeros((1,), jnp.float32)], 0)
    send_x = padded_x[token_of].reshape(experts, capacity, width_part)
    send_dy = (padded_dy[token_of].astype(jnp.float32) * padded_p[table][:, None]).astype(
        jnp.bfloat16
    )
    send_dy = send_dy.reshape(experts, capacity, width_part)
    gate_mat = w_gate[0]
    up_mat = w_up[0]
    down_mat = w_down[0]
    recv_x, recv_dy = (
        lax.all_to_all(send_x, "ep", split_axis=0, concat_axis=0, tiled=True),
        lax.all_to_all(send_dy, "ep", split_axis=0, concat_axis=0, tiled=True),
    )
    recv_x = recv_x.reshape(-1, width_part)
    recv_dy = recv_dy.reshape(-1, width_part)
    gate_part = jnp.dot(recv_x, gate_mat, preferred_element_type=jnp.float32)
    up_part = jnp.dot(recv_x, up_mat, preferred_element_type=jnp.float32)
    dact_part = contract_cols(recv_dy, down_mat)
    gate, up, dact = (
        lax.psum(gate_part.astype(jnp.bfloat16), "tp").astype(jnp.float32),
        lax.psum(up_part.astype(jnp.bfloat16), "tp").astype(jnp.float32),
        lax.psum(dact_part.astype(jnp.bfloat16), "tp").astype(jnp.float32),
    )
    act, dgate, dup = swiglu_back(gate, up, dact)
    dx_rows = (contract_cols(dgate, gate_mat) + contract_cols(dup, up_mat)).astype(jnp.bfloat16)
    returned = lax.all_to_all(
        dx_rows.reshape(experts, capacity, width_part),
        "ep",
        split_axis=0,
        concat_axis=0,
        tiled=True,
    )
    scale = 1.0 / tok_rows
    x_sq = squared(recv_x)
    fisher_gate = (contract_rows(x_sq, squared(dgate)) * scale).astype(jnp.bfloat16)[None]
    fisher_up = (contract_rows(x_sq, squared(dup)) * scale).astype(jnp.bfloat16)[None]
    fisher_down = (contract_rows(squared(act), squared(recv_dy)) * scale).astype(jnp.bfloat16)[None]
    pulled = returned.reshape(experts * capacity, width_part)[slot_index].astype(jnp.float32)
    grad_tokens = jnp.sum(pulled.reshape(tok_rows, top_count, width_part), 1).astype(jnp.bfloat16)
    return (grad_tokens, fisher_gate, fisher_up, fisher_down)


MESH = pl.DeviceIdType.MESH
F32 = jnp.float32
BF16 = jnp.bfloat16
ROW_TILE = 16
LANES = 128
VMEM_BYTES = 60 * 1024 * 1024


def flipped(index, mask):
    out, bit = index, 1
    while bit <= mask:
        if mask & bit:
            out = out + bit * (1 - 2 * ((index // bit) % 2))
        bit *= 2
    return out


def slot_rows(tok_rows, top_count, experts):
    capacity = tok_rows * top_count * 9 // (8 * experts)
    return -(-capacity // ROW_TILE) * ROW_TILE


def fused_kernel(
    n_ep, n_tp, rows,
    tok_ref, og_ref, pe_ref, wg_hbm, wu_hbm, wd_hbm,
    grad_ref, fg_hbm, fu_hbm, fd_hbm,
    wg, wu, wd, rank, onehot, peb, tb, sx, rx, pb, rb, sb, rb2, af, dxs, ret, tsq, sqb, fg, fu, fd,
    w_sem, o_sem, pes_sem, per_sem, ts_sem, tr_sem, xs_sem, xr_sem,
    ps_sem, pr_sem, qs_sem, qr_sem, as_sem, ar_sem, ds_sem, dr_sem,
):
    e = lax.axis_index("ep")
    q = lax.axis_index("tp")
    row, mate = e // 2, flipped(e, 1)
    tok_rows, width = tok_ref.shape
    ff = wg.shape[1]
    half = ff // 2
    pair = 2 * rows
    chunks = n_ep // 2
    scale = 1.0 / tok_rows
    blocks = (tok_ref, og_ref)

    loads = [
        pltpu.make_async_copy(hbm.at[0], vmem, w_sem.at[i])
        for i, (hbm, vmem) in enumerate(((wg_hbm, wg), (wu_hbm, wu), (wd_hbm, wd)))
    ]
    for copy in loads:
        copy.start()

    barrier = pltpu.get_barrier_semaphore()
    for k in range(1, n_ep):
        pl.semaphore_signal(barrier, inc=1, device_id=(flipped(e, k), q), device_id_type=MESH)
    for j in range(1, n_tp):
        pl.semaphore_signal(barrier, inc=1, device_id=(e, flipped(q, j)), device_id_type=MESH)
    before = (
        lax.broadcasted_iota(jnp.int32, (tok_rows, tok_rows), 0)
        < lax.broadcasted_iota(jnp.int32, (tok_rows, tok_rows), 1)
    ).astype(BF16)
    slot_iota = lax.broadcasted_iota(jnp.int32, (rows, tok_rows), 0)
    pl.semaphore_wait(barrier, n_ep + n_tp - 2)

    def remote(src, dst, send_sem, recv_sem, device):
        return pltpu.make_async_remote_copy(
            src_ref=src,
            dst_ref=dst,
            send_sem=send_sem,
            recv_sem=recv_sem,
            device_id=device,
            device_id_type=MESH,
        )

    def block(k):
        return pl.ds(k * rows, rows)

    def hop(direction, distance, i):
        step = 1 - 2 * direction
        source = row - step * distance
        src = blocks[i] if distance == 0 else tb.at[source, i]
        return remote(
            src,
            tb.at[source, i],
            ts_sem.at[direction, distance, i],
            tr_sem.at[direction, distance, i],
            (e + 2 * step, q),
        )

    def sends(direction, distance):
        if direction == 0:
            return (row >= distance) & (row < chunks - 1)
        return (row + distance < chunks) & (row > 0)

    def holds(direction, distance):
        if direction == 0:
            return row >= distance
        return row + distance < chunks

    def landed(direction, distance, i):
        source = row - (1 - 2 * direction) * distance
        return remote(
            tb.at[source, i],
            tb.at[source, i],
            ts_sem.at[direction, distance - 1, i],
            tr_sem.at[direction, distance - 1, i],
            (mate, q),
        )

    def arrive(distance):
        for i in range(2):
            for direction in range(2):
                if distance:

                    @pl.when(holds(direction, distance))
                    def _():
                        landed(direction, distance, i).wait_recv()

                if distance < chunks - 1:

                    @pl.when(sends(direction, distance))
                    def _():
                        hop(direction, distance, i).start()

    pe_copies = [None] * chunks

    def send_probs():
        for c in range(1, chunks):
            pe_copies[c] = remote(
                pe_ref, peb.at[row], pes_sem.at[c], per_sem.at[c], (flipped(e, 2 * c), q)
            )
            pe_copies[c].start()

    def ranked(probs):
        mask = (probs > 0.0).astype(F32)
        ranks = jnp.dot(mask.astype(BF16), before, preferred_element_type=F32)
        rank[...] = jnp.where(mask > 0.0, ranks, -1.0).astype(jnp.int32)

    x_copies = [None] * chunks

    def select(c):
        source = flipped(row, c)
        if c:
            pe_copies[c].wait_recv()
            probs, pair_of = peb.at[source], (tb.at[source, 0], tb.at[source, 1])
        else:
            probs, pair_of = pe_ref, blocks
        ranked(probs[...])
        for dest, out, k in ((mate, sx, c), (e, rx, 2 * c)):
            hot = (slot_iota == rank[pl.ds(dest, 1), :]).astype(F32)
            hot16 = hot.astype(BF16)
            prob = jnp.sum(hot * probs[pl.ds(dest, 1), :], 1, keepdims=True)
            out[0, block(k), :] = jnp.dot(
                hot16, pair_of[0][...], preferred_element_type=F32
            ).astype(BF16)
            out[1, block(k), :] = (
                jnp.dot(hot16, pair_of[1][...], preferred_element_type=F32) * prob
            ).astype(BF16)
            if out is sx:
                x_copies[c] = remote(
                    sx.at[:, block(c), :],
                    rx.at[:, block(2 * c + 1), :],
                    xs_sem.at[c],
                    xr_sem.at[c],
                    (mate, q),
                )
                x_copies[c].start()

    def own_onehot():
        ranked(pe_ref[...])
        for k in range(n_ep):
            onehot[block(k), :] = (slot_iota == rank[pl.ds(flipped(e, k), 1), :]).astype(F32).astype(BF16)

    def piece(index):
        return (
            pl.ds(pl.multiple_of((index // 2) * rows, ROW_TILE), rows),
            pl.ds(pl.multiple_of((index % 2) * half, LANES), half),
        )

    def placed(c, index):
        r = pl.ds(pl.multiple_of(c * pair + (index // 2) * rows, ROW_TILE), rows)
        return af.at[:, r, piece(index)[1]]

    near, far = flipped(q, 1), flipped(q, 2)
    p_copies = [None] * chunks
    q_copies = [None] * chunks
    a_copies = [None] * chunks
    d_copies = [None] * n_ep

    def partials(c):
        span = pl.ds(c * pair, pair)
        x_copies[c].wait_recv()
        if c == 0:
            for copy in loads:
                copy.wait()
        x = rx[0, span, :]
        pb[c, 0] = jnp.dot(x, wg[...], preferred_element_type=F32).astype(BF16)
        pb[c, 1] = jnp.dot(x, wu[...], preferred_element_type=F32).astype(BF16)
        pb[c, 2] = contract_cols(rx[1, span, :], wd[...]).astype(BF16)
        p_copies[c] = []
        for j, other in enumerate((near, flipped(q, 3))):
            r, l = piece(other)
            copy = remote(
                pb.at[c, :, r, l],
                rb.at[c, j],
                ps_sem.at[c, j],
                pr_sem.at[c, j],
                (e, near),
            )
            copy.start()
            p_copies[c].append(copy)

    def pair_sum(c):
        p_copies[c][1].wait_recv()
        r, l = piece(far)
        for i in range(3):
            sb[c, i] = (pb[c, i, r, l].astype(F32) + rb[c, 1, i].astype(F32)).astype(BF16)
        q_copies[c] = remote(sb.at[c], rb2.at[c], qs_sem.at[c], qr_sem.at[c], (e, far))
        q_copies[c].start()

    def activate(c):
        p_copies[c][0].wait_recv()
        q_copies[c].wait_recv()
        r, l = piece(q)
        gate, up, dact = [
            pb[c, i, r, l].astype(F32) + rb[c, 0, i].astype(F32) + rb2[c, i].astype(F32)
            for i in range(3)
        ]
        r = pl.ds(pl.multiple_of(c * pair + (q // 2) * rows, ROW_TILE), rows)
        for i, value in enumerate(swiglu_back(gate, up, dact)):
            af[i, r, l] = value
        mine = placed(c, q)
        a_copies[c] = [
            remote(mine, mine, as_sem.at[c, j], ar_sem.at[c, j], (e, other))
            for j, other in enumerate((far, near))
        ]
        for copy in a_copies[c]:
            copy.start()

    def relay(c):
        theirs = placed(c, far)
        remote(theirs, theirs, as_sem.at[c, 0], ar_sem.at[c, 0], (e, far)).wait_recv()
        copy = remote(theirs, theirs, as_sem.at[c, 2], ar_sem.at[c, 2], (e, near))
        copy.start()
        a_copies[c].append(copy)

    def input_grad(c):
        for j, index in ((1, near), (2, flipped(q, 3))):
            theirs = placed(c, index)
            remote(theirs, theirs, as_sem.at[c, j], ar_sem.at[c, j], (e, near)).wait_recv()
        span = pl.ds(c * pair, pair)
        dx = contract_cols(af[1, span, :], wg[...]) + contract_cols(af[2, span, :], wu[...])
        dxs[span, :] = dx.astype(BF16)
        for k in (2 * c, 2 * c + 1):
            if k:
                d_copies[k] = remote(
                    dxs.at[block(k), :],
                    ret.at[block(k), :],
                    ds_sem.at[k],
                    dr_sem.at[k],
                    (flipped(e, k), q),
                )
                d_copies[k].start()
            else:
                ret[block(0), :] = dxs[block(0), :]

    def transposed_squares(source, i, columns):
        @pl.loop(0, columns // LANES)
        def _(step):
            l = pl.ds(pl.multiple_of(step * LANES, LANES), LANES)
            tsq[l, :] = squared(source[i, :, l]).T

    def fisher(columns, depth, out):
        @pl.loop(0, columns // LANES)
        def _(step):
            r = pl.ds(pl.multiple_of(step * LANES, LANES), LANES)
            sums = jnp.dot(tsq[r, :], sqb[:, :depth], preferred_element_type=F32)
            out[r, :] = (sums * scale).astype(BF16)

    stores = []

    def store(i, vmem, hbm):
        copy = pltpu.make_async_copy(vmem, hbm.at[0], o_sem.at[i])
        copy.start()
        stores.append(copy)

    arrive(0)
    send_probs()
    for c in range(chunks):
        if c:
            arrive(c)
            activate(c - 1)
        select(c)
        partials(c)
        if c:
            relay(c - 1)
        pair_sum(c)
        if c:
            input_grad(c - 1)
    last = chunks - 1
    transposed_squares(rx, 0, width)
    activate(last)
    relay(last)
    own_onehot()
    input_grad(last)
    sqb[:, :ff] = squared(af[1])
    fisher(width, ff, fg)
    store(0, fg, fg_hbm)
    sqb[:, :ff] = squared(af[2])
    fisher(width, ff, fu)
    store(1, fu, fu_hbm)
    transposed_squares(af, 0, ff)
    sqb[...] = squared(rx[1])
    fisher(ff, width, fd)
    store(2, fd, fd_hbm)

    for k in range(1, n_ep):
        d_copies[k].wait_recv()
    grad_ref[...] = contract_rows(onehot[...], ret[...]).astype(BF16)

    for distance in range(chunks - 1):
        for direction in range(2):

            @pl.when(sends(direction, distance))
            def _():
                for i in range(2):
                    hop(direction, distance, i).wait_send()

    for copy in pe_copies[1:] + x_copies + q_copies + d_copies[1:] + sum(p_copies + a_copies, []):
        copy.wait_send()
    for copy in stores:
        copy.wait()


def fused_on_device(n_ep, n_tp, tokens, out_grad, expert_ids, route_probs, w_gate, w_up, w_down):
    tok_rows, width = tokens.shape
    ff = w_gate.shape[2]
    rows = slot_rows(tok_rows, expert_ids.shape[1], n_ep)
    total, chunks = n_ep * rows, n_ep // 2
    names = jnp.arange(n_ep, dtype=jnp.int32)[:, None, None]
    probs = jnp.sum(jnp.where(expert_ids[None] == names, route_probs[None], 0.0), 2)
    any_spec = pl.BlockSpec(memory_space=pl.ANY)
    vmem_spec = pl.BlockSpec(memory_space=pltpu.VMEM)
    dma = pltpu.SemaphoreType.DMA
    return pl.pallas_call(
        functools.partial(fused_kernel, n_ep, n_tp, rows),
        out_shape=(
            jax.ShapeDtypeStruct(tokens.shape, BF16),
            jax.ShapeDtypeStruct(w_gate.shape, BF16),
            jax.ShapeDtypeStruct(w_up.shape, BF16),
            jax.ShapeDtypeStruct(w_down.shape, BF16),
        ),
        in_specs=[vmem_spec] * 3 + [any_spec] * 3,
        out_specs=[vmem_spec] + [any_spec] * 3,
        scratch_shapes=[
            pltpu.VMEM((width, ff), BF16),
            pltpu.VMEM((width, ff), BF16),
            pltpu.VMEM((ff, width), BF16),
            pltpu.VMEM((n_ep, tok_rows), jnp.int32),
            pltpu.VMEM((total, tok_rows), BF16),
            pltpu.VMEM((chunks, n_ep, tok_rows), F32),
            pltpu.VMEM((chunks, 2, tok_rows, width), BF16),
            pltpu.VMEM((2, total // 2, width), BF16),
            pltpu.VMEM((2, total, width), BF16),
            pltpu.VMEM((chunks, 3, 2 * rows, ff), BF16),
            pltpu.VMEM((chunks, 2, 3, rows, ff // 2), BF16),
            pltpu.VMEM((chunks, 3, rows, ff // 2), BF16),
            pltpu.VMEM((chunks, 3, rows, ff // 2), BF16),
            pltpu.VMEM((3, total, ff), BF16),
            pltpu.VMEM((total, width), BF16),
            pltpu.VMEM((total, width), BF16),
            pltpu.VMEM((width, total), BF16),
            pltpu.VMEM((total, width), BF16),
            pltpu.VMEM((width, ff), BF16),
            pltpu.VMEM((width, ff), BF16),
            pltpu.VMEM((ff, width), BF16),
            dma((3,)),
            dma((3,)),
            dma((chunks,)),
            dma((chunks,)),
            dma((2, chunks, 2)),
            dma((2, chunks, 2)),
            dma((chunks,)),
            dma((chunks,)),
            dma((chunks, 2)),
            dma((chunks, 2)),
            dma((chunks,)),
            dma((chunks,)),
            dma((chunks, 3)),
            dma((chunks, 3)),
            dma((n_ep,)),
            dma((n_ep,)),
        ],
        compiler_params=pltpu.CompilerParams(
            collective_id=0, has_side_effects=True, vmem_limit_bytes=VMEM_BYTES
        ),
    )(tokens, out_grad, probs, w_gate, w_up, w_down)


def part(n_ep, n_tp, *args):
    tokens, expert_ids, w_gate = args[0], args[2], args[4]
    width, ff = w_gate.shape[1:]
    rows = slot_rows(tokens.shape[0], expert_ids.shape[1], n_ep)
    fits = (
        n_tp == 4
        and n_ep in (4, 8)
        and ff <= width
        and ff % (2 * LANES) == 0
        and width % LANES == 0
        and n_ep * rows * (17 * width + 18 * ff) + 14 * width * ff < VMEM_BYTES
    )
    if fits:
        return fused_on_device(n_ep, n_tp, *args)
    return on_device(*args)


def solution(mesh):
    in_specs = (
        P("ep", "tp"),
        P("ep", "tp"),
        P("ep", None),
        P("ep", None),
        P("ep", "tp", None),
        P("ep", "tp", None),
        P("ep", None, "tp"),
    )
    out_specs = (P("ep", "tp"), P("ep", "tp", None), P("ep", "tp", None), P("ep", None, "tp"))
    return jax.shard_map(
        functools.partial(part, mesh.shape["ep"], mesh.shape["tp"]), mesh=mesh, in_specs=in_specs, out_specs=out_specs, check_vma=False
    )
```

```python
import functools

import jax
import jax.numpy as jnp
from jax import lax
from jax.experimental import pallas as pl
from jax.experimental.pallas import tpu as pltpu
from jax.sharding import PartitionSpec as P


def contract_rows(left, right):
    return lax.dot_general(
        left, right, (((0,), (0,)), ((), ())), preferred_element_type=jnp.float32
    )


def contract_cols(left, right):
    return lax.dot_general(
        left, right, (((1,), (1,)), ((), ())), preferred_element_type=jnp.float32
    )


def swiglu_back(gate, up, dact):
    sig = jax.nn.sigmoid(gate)
    act = (gate * sig * up).astype(jnp.bfloat16)
    dgate = (dact * up * sig * (1.0 + gate * (1.0 - sig))).astype(jnp.bfloat16)
    dup = (dact * gate * sig).astype(jnp.bfloat16)
    return (act, dgate, dup)


def squared(values):
    return jnp.square(values.astype(jnp.float32)).astype(jnp.bfloat16)


def on_device(tokens, out_grad, expert_ids, route_probs, w_gate, w_up, w_down):
    tok_rows = tokens.shape[0]
    width_part = tokens.shape[1]
    top_count = expert_ids.shape[1]
    experts = lax.axis_size("ep")
    capacity = tok_rows * top_count * 9 // (8 * experts)
    assigns = tok_rows * top_count
    flat_ids = expert_ids.reshape(-1)
    onehot = (flat_ids[:, None] == jnp.arange(experts, dtype=jnp.int32)[None, :]).astype(jnp.int32)
    ranks = jnp.sum((jnp.cumsum(onehot, 0) - onehot) * onehot, 1)
    slot_index = flat_ids * capacity + ranks
    table = (
        jnp.full((experts * capacity,), assigns, jnp.int32)
        .at[slot_index]
        .set(jnp.arange(assigns, dtype=jnp.int32))
    )
    token_of = table // top_count
    padded_x = jnp.concatenate([tokens, jnp.zeros((1, width_part), tokens.dtype)], 0)
    padded_dy = jnp.concatenate([out_grad, jnp.zeros((1, width_part), out_grad.dtype)], 0)
    padded_p = jnp.concatenate([route_probs.reshape(-1), jnp.zeros((1,), jnp.float32)], 0)
    send_x = padded_x[token_of].reshape(experts, capacity, width_part)
    send_dy = (padded_dy[token_of].astype(jnp.float32) * padded_p[table][:, None]).astype(
        jnp.bfloat16
    )
    send_dy = send_dy.reshape(experts, capacity, width_part)
    gate_mat = w_gate[0]
    up_mat = w_up[0]
    down_mat = w_down[0]
    recv_x, recv_dy = (
        lax.all_to_all(send_x, "ep", split_axis=0, concat_axis=0, tiled=True),
        lax.all_to_all(send_dy, "ep", split_axis=0, concat_axis=0, tiled=True),
    )
    recv_x = recv_x.reshape(-1, width_part)
    recv_dy = recv_dy.reshape(-1, width_part)
    gate_part = jnp.dot(recv_x, gate_mat, preferred_element_type=jnp.float32)
    up_part = jnp.dot(recv_x, up_mat, preferred_element_type=jnp.float32)
    dact_part = contract_cols(recv_dy, down_mat)
    gate, up, dact = (
        lax.psum(gate_part.astype(jnp.bfloat16), "tp").astype(jnp.float32),
        lax.psum(up_part.astype(jnp.bfloat16), "tp").astype(jnp.float32),
        lax.psum(dact_part.astype(jnp.bfloat16), "tp").astype(jnp.float32),
    )
    act, dgate, dup = swiglu_back(gate, up, dact)
    dx_rows = (contract_cols(dgate, gate_mat) + contract_cols(dup, up_mat)).astype(jnp.bfloat16)
    returned = lax.all_to_all(
        dx_rows.reshape(experts, capacity, width_part),
        "ep",
        split_axis=0,
        concat_axis=0,
        tiled=True,
    )
    scale = 1.0 / tok_rows
    x_sq = squared(recv_x)
    fisher_gate = (contract_rows(x_sq, squared(dgate)) * scale).astype(jnp.bfloat16)[None]
    fisher_up = (contract_rows(x_sq, squared(dup)) * scale).astype(jnp.bfloat16)[None]
    fisher_down = (contract_rows(squared(act), squared(recv_dy)) * scale).astype(jnp.bfloat16)[None]
    pulled = returned.reshape(experts * capacity, width_part)[slot_index].astype(jnp.float32)
    grad_tokens = jnp.sum(pulled.reshape(tok_rows, top_count, width_part), 1).astype(jnp.bfloat16)
    return (grad_tokens, fisher_gate, fisher_up, fisher_down)


MESH = pl.DeviceIdType.MESH
F32 = jnp.float32
BF16 = jnp.bfloat16
ROW_TILE = 16
LANES = 128
VMEM_BYTES = 36 * 1024 * 1024


def flipped(index, mask):
    out, bit = index, 1
    while bit <= mask:
        if mask & bit:
            out = out + bit * (1 - 2 * ((index // bit) % 2))
        bit *= 2
    return out


def slot_rows(tok_rows, top_count, experts):
    capacity = tok_rows * top_count * 9 // (8 * experts)
    return -(-capacity // ROW_TILE) * ROW_TILE


def fused_kernel(
    n_ep, n_tp, rows,
    tok_ref, og_ref, pe_ref, wg_hbm, wu_hbm, wd_hbm,
    grad_ref, fg_hbm, fu_hbm, fd_hbm,
    wg, wu, wd, rank, onehot, peb, tb, sx, rx, pb, rb, sb, rb2, af, dxs, ret, tsq, sqb, fg, fu, fd,
    w_sem, o_sem, pes_sem, per_sem, ts_sem, tr_sem, xs_sem, xr_sem,
    ps_sem, pr_sem, qs_sem, qr_sem, as_sem, ar_sem, ds_sem, dr_sem,
):
    e = lax.axis_index("ep")
    q = lax.axis_index("tp")
    row, mate = e // 2, flipped(e, 1)
    tok_rows, width = tok_ref.shape
    ff = wg.shape[1]
    half = ff // 2
    pair = 2 * rows
    chunks = n_ep // 2
    scale = 1.0 / tok_rows
    blocks = (tok_ref, og_ref)

    loads = [
        pltpu.make_async_copy(hbm.at[0], vmem, w_sem.at[i])
        for i, (hbm, vmem) in enumerate(((wg_hbm, wg), (wu_hbm, wu), (wd_hbm, wd)))
    ]
    for copy in loads:
        copy.start()

    barrier = pltpu.get_barrier_semaphore()
    for k in range(1, n_ep):
        pl.semaphore_signal(barrier, inc=1, device_id=(flipped(e, k), q), device_id_type=MESH)
    for j in range(1, n_tp):
        pl.semaphore_signal(barrier, inc=1, device_id=(e, flipped(q, j)), device_id_type=MESH)
    before = (
        lax.broadcasted_iota(jnp.int32, (tok_rows, tok_rows), 0)
        < lax.broadcasted_iota(jnp.int32, (tok_rows, tok_rows), 1)
    ).astype(BF16)
    slot_iota = lax.broadcasted_iota(jnp.int32, (rows, tok_rows), 0)
    pl.semaphore_wait(barrier, n_ep + n_tp - 2)

    def remote(src, dst, send_sem, recv_sem, device):
        return pltpu.make_async_remote_copy(
            src_ref=src,
            dst_ref=dst,
            send_sem=send_sem,
            recv_sem=recv_sem,
            device_id=device,
            device_id_type=MESH,
        )

    def block(k):
        return pl.ds(k * rows, rows)

    def hop(direction, distance, i):
        step = 1 - 2 * direction
        source = row - step * distance
        src = blocks[i] if distance == 0 else tb.at[source, i]
        return remote(
            src,
            tb.at[source, i],
            ts_sem.at[direction, distance, i],
            tr_sem.at[direction, distance, i],
            (e + 2 * step, q),
        )

    def sends(direction, distance):
        if direction == 0:
            return (row >= distance) & (row < chunks - 1)
        return (row + distance < chunks) & (row > 0)

    def holds(direction, distance):
        if direction == 0:
            return row >= distance
        return row + distance < chunks

    def landed(direction, distance, i):
        source = row - (1 - 2 * direction) * distance
        return remote(
            tb.at[source, i],
            tb.at[source, i],
            ts_sem.at[direction, distance - 1, i],
            tr_sem.at[direction, distance - 1, i],
            (mate, q),
        )

    def arrive(distance, i):
        for direction in range(2):
            if distance:

                @pl.when(holds(direction, distance))
                def _():
                    landed(direction, distance, i).wait_recv()

            if distance < chunks - 1:

                @pl.when(sends(direction, distance))
                def _():
                    hop(direction, distance, i).start()

    pe_copies = [None] * chunks

    def send_probs():
        for c in range(1, chunks):
            pe_copies[c] = remote(
                pe_ref, peb.at[row], pes_sem.at[c], per_sem.at[c], (flipped(e, 2 * c), q)
            )
            pe_copies[c].start()

    def ranked(probs):
        mask = (probs > 0.0).astype(F32)
        ranks = jnp.dot(mask.astype(BF16), before, preferred_element_type=F32)
        rank[...] = jnp.where(mask > 0.0, ranks, -1.0).astype(jnp.int32)

    x_copies = [[None, None] for _ in range(chunks)]

    def select(c, i):
        source = flipped(row, c)
        if c:
            if i == 0:
                pe_copies[c].wait_recv()
            probs, rows_of = peb.at[source], tb.at[source, i]
        else:
            probs, rows_of = pe_ref, blocks[i]
        if i == 0:
            ranked(probs[...])
        for dest, out, k in ((mate, sx, c), (e, rx, 2 * c)):
            hot = (slot_iota == rank[pl.ds(dest, 1), :]).astype(F32)
            picked = jnp.dot(hot.astype(BF16), rows_of[...], preferred_element_type=F32)
            if i:
                picked = picked * jnp.sum(hot * probs[pl.ds(dest, 1), :], 1, keepdims=True)
            out[i, block(k), :] = picked.astype(BF16)
            if out is sx:
                x_copies[c][i] = remote(
                    sx.at[i, block(c), :],
                    rx.at[i, block(2 * c + 1), :],
                    xs_sem.at[c, i],
                    xr_sem.at[c, i],
                    (mate, q),
                )
                x_copies[c][i].start()

    def own_onehot():
        ranked(pe_ref[...])
        for k in range(n_ep):
            onehot[block(k), :] = (slot_iota == rank[pl.ds(flipped(e, k), 1), :]).astype(F32).astype(BF16)

    def piece(index):
        return (
            pl.ds(pl.multiple_of((index // 2) * rows, ROW_TILE), rows),
            pl.ds(pl.multiple_of((index % 2) * half, LANES), half),
        )

    def placed(c, index):
        r = pl.ds(pl.multiple_of(c * pair + (index // 2) * rows, ROW_TILE), rows)
        return af.at[:, r, piece(index)[1]]

    near, far = flipped(q, 1), flipped(q, 2)
    p_copies = [None] * chunks
    q_copies = [None] * chunks
    a_copies = [None] * chunks
    d_copies = [None] * n_ep

    def partials(c):
        span = pl.ds(c * pair, pair)
        x_copies[c][0].wait_recv()
        if c == 0:
            for copy in loads:
                copy.wait()
        x = rx[0, span, :]
        pb[c, 0] = jnp.dot(x, wg[...], preferred_element_type=F32).astype(BF16)
        pb[c, 1] = jnp.dot(x, wu[...], preferred_element_type=F32).astype(BF16)
        x_copies[c][1].wait_recv()
        pb[c, 2] = contract_cols(rx[1, span, :], wd[...]).astype(BF16)
        p_copies[c] = []
        for j, other in enumerate((near, flipped(q, 3))):
            r, l = piece(other)
            copy = remote(
                pb.at[c, :, r, l],
                rb.at[c, j],
                ps_sem.at[c, j],
                pr_sem.at[c, j],
                (e, near),
            )
            copy.start()
            p_copies[c].append(copy)

    def pair_sum(c):
        p_copies[c][1].wait_recv()
        r, l = piece(far)
        for i in range(3):
            sb[c, i] = (pb[c, i, r, l].astype(F32) + rb[c, 1, i].astype(F32)).astype(BF16)
        q_copies[c] = remote(sb.at[c], rb2.at[c], qs_sem.at[c], qr_sem.at[c], (e, far))
        q_copies[c].start()

    def activate(c):
        p_copies[c][0].wait_recv()
        q_copies[c].wait_recv()
        r, l = piece(q)
        gate, up, dact = [
            pb[c, i, r, l].astype(F32) + rb[c, 0, i].astype(F32) + rb2[c, i].astype(F32)
            for i in range(3)
        ]
        r = pl.ds(pl.multiple_of(c * pair + (q // 2) * rows, ROW_TILE), rows)
        for i, value in enumerate(swiglu_back(gate, up, dact)):
            af[i, r, l] = value
        mine = placed(c, q)
        a_copies[c] = [
            remote(mine, mine, as_sem.at[c, j], ar_sem.at[c, j], (e, other))
            for j, other in enumerate((far, near))
        ]
        for copy in a_copies[c]:
            copy.start()

    def relay(c):
        theirs = placed(c, far)
        remote(theirs, theirs, as_sem.at[c, 0], ar_sem.at[c, 0], (e, far)).wait_recv()
        copy = remote(theirs, theirs, as_sem.at[c, 2], ar_sem.at[c, 2], (e, near))
        copy.start()
        a_copies[c].append(copy)

    def input_grad(c):
        for j, index in ((1, near), (2, flipped(q, 3))):
            theirs = placed(c, index)
            remote(theirs, theirs, as_sem.at[c, j], ar_sem.at[c, j], (e, near)).wait_recv()
        span = pl.ds(c * pair, pair)
        dx = contract_cols(af[1, span, :], wg[...]) + contract_cols(af[2, span, :], wu[...])
        dxs[span, :] = dx.astype(BF16)
        for k in (2 * c, 2 * c + 1):
            if k:
                d_copies[k] = remote(
                    dxs.at[block(k), :],
                    ret.at[block(k), :],
                    ds_sem.at[k],
                    dr_sem.at[k],
                    (flipped(e, k), q),
                )
                d_copies[k].start()
            else:
                ret[block(0), :] = dxs[block(0), :]

    def transposed_squares(source, i, columns):
        @pl.loop(0, columns // LANES)
        def _(step):
            l = pl.ds(pl.multiple_of(step * LANES, LANES), LANES)
            tsq[l, :] = squared(source[i, :, l]).T

    def fisher(columns, depth, out):
        @pl.loop(0, columns // LANES)
        def _(step):
            r = pl.ds(pl.multiple_of(step * LANES, LANES), LANES)
            sums = jnp.dot(tsq[r, :], sqb[:, :depth], preferred_element_type=F32)
            out[r, :] = (sums * scale).astype(BF16)

    stores = []

    def store(i, vmem, hbm):
        copy = pltpu.make_async_copy(vmem, hbm.at[0], o_sem.at[i])
        copy.start()
        stores.append(copy)

    arrive(0, 0)
    send_probs()
    arrive(0, 1)
    for c in range(chunks):
        if c:
            arrive(c, 0)
        select(c, 0)
        if c:
            activate(c - 1)
            arrive(c, 1)
        select(c, 1)
        partials(c)
        if c:
            relay(c - 1)
        pair_sum(c)
        if c:
            input_grad(c - 1)
    last = chunks - 1
    transposed_squares(rx, 0, width)
    activate(last)
    relay(last)
    own_onehot()
    input_grad(last)
    sqb[:, :ff] = squared(af[1])
    fisher(width, ff, fg)
    store(0, fg, fg_hbm)
    sqb[:, :ff] = squared(af[2])
    fisher(width, ff, fu)
    store(1, fu, fu_hbm)
    transposed_squares(af, 0, ff)
    sqb[...] = squared(rx[1])
    fisher(ff, width, fd)
    store(2, fd, fd_hbm)

    for k in range(1, n_ep):
        d_copies[k].wait_recv()
    grad_ref[...] = contract_rows(onehot[...], ret[...]).astype(BF16)

    for distance in range(chunks - 1):
        for direction in range(2):

            @pl.when(sends(direction, distance))
            def _():
                for i in range(2):
                    hop(direction, distance, i).wait_send()

    for copy in pe_copies[1:] + q_copies + d_copies[1:] + sum(x_copies + p_copies + a_copies, []):
        copy.wait_send()
    for copy in stores:
        copy.wait()


def fused_on_device(n_ep, n_tp, tokens, out_grad, expert_ids, route_probs, w_gate, w_up, w_down):
    tok_rows, width = tokens.shape
    ff = w_gate.shape[2]
    rows = slot_rows(tok_rows, expert_ids.shape[1], n_ep)
    total, chunks = n_ep * rows, n_ep // 2
    names = jnp.arange(n_ep, dtype=jnp.int32)[:, None, None]
    probs = jnp.sum(jnp.where(expert_ids[None] == names, route_probs[None], 0.0), 2)
    any_spec = pl.BlockSpec(memory_space=pl.ANY)
    vmem_spec = pl.BlockSpec(memory_space=pltpu.VMEM)
    dma = pltpu.SemaphoreType.DMA
    return pl.pallas_call(
        functools.partial(fused_kernel, n_ep, n_tp, rows),
        out_shape=(
            jax.ShapeDtypeStruct(tokens.shape, BF16),
            jax.ShapeDtypeStruct(w_gate.shape, BF16),
            jax.ShapeDtypeStruct(w_up.shape, BF16),
            jax.ShapeDtypeStruct(w_down.shape, BF16),
        ),
        in_specs=[vmem_spec] * 3 + [any_spec] * 3,
        out_specs=[vmem_spec] + [any_spec] * 3,
        scratch_shapes=[
            pltpu.VMEM((width, ff), BF16),
            pltpu.VMEM((width, ff), BF16),
            pltpu.VMEM((ff, width), BF16),
            pltpu.VMEM((n_ep, tok_rows), jnp.int32),
            pltpu.VMEM((total, tok_rows), BF16),
            pltpu.VMEM((chunks, n_ep, tok_rows), F32),
            pltpu.VMEM((chunks, 2, tok_rows, width), BF16),
            pltpu.VMEM((2, total // 2, width), BF16),
            pltpu.VMEM((2, total, width), BF16),
            pltpu.VMEM((chunks, 3, 2 * rows, ff), BF16),
            pltpu.VMEM((chunks, 2, 3, rows, ff // 2), BF16),
            pltpu.VMEM((chunks, 3, rows, ff // 2), BF16),
            pltpu.VMEM((chunks, 3, rows, ff // 2), BF16),
            pltpu.VMEM((3, total, ff), BF16),
            pltpu.VMEM((total, width), BF16),
            pltpu.VMEM((total, width), BF16),
            pltpu.VMEM((width, total), BF16),
            pltpu.VMEM((total, width), BF16),
            pltpu.VMEM((width, ff), BF16),
            pltpu.VMEM((width, ff), BF16),
            pltpu.VMEM((ff, width), BF16),
            dma((3,)),
            dma((3,)),
            dma((chunks,)),
            dma((chunks,)),
            dma((2, chunks, 2)),
            dma((2, chunks, 2)),
            dma((chunks, 2)),
            dma((chunks, 2)),
            dma((chunks, 2)),
            dma((chunks, 2)),
            dma((chunks,)),
            dma((chunks,)),
            dma((chunks, 3)),
            dma((chunks, 3)),
            dma((n_ep,)),
            dma((n_ep,)),
        ],
        compiler_params=pltpu.CompilerParams(
            collective_id=0, has_side_effects=True, vmem_limit_bytes=VMEM_BYTES
        ),
    )(tokens, out_grad, probs, w_gate, w_up, w_down)


def part(n_ep, n_tp, *args):
    tokens, expert_ids, w_gate = args[0], args[2], args[4]
    width, ff = w_gate.shape[1:]
    rows = slot_rows(tokens.shape[0], expert_ids.shape[1], n_ep)
    fits = (
        n_tp == 4
        and n_ep in (4, 8)
        and ff <= width
        and ff % (2 * LANES) == 0
        and width % LANES == 0
        and n_ep * rows * (17 * width + 18 * ff) + 14 * width * ff < VMEM_BYTES
    )
    if fits:
        return fused_on_device(n_ep, n_tp, *args)
    return on_device(*args)


def solution(mesh):
    in_specs = (
        P("ep", "tp"),
        P("ep", "tp"),
        P("ep", None),
        P("ep", None),
        P("ep", "tp", None),
        P("ep", "tp", None),
        P("ep", None, "tp"),
    )
    out_specs = (P("ep", "tp"), P("ep", "tp", None), P("ep", "tp", None), P("ep", None, "tp"))
    return jax.shard_map(
        functools.partial(part, mesh.shape["ep"], mesh.shape["tp"]), mesh=mesh, in_specs=in_specs, out_specs=out_specs, check_vma=False
    )
```

```python
import functools

import jax
import jax.numpy as jnp
from jax import lax
from jax.experimental import pallas as pl
from jax.experimental.pallas import tpu as pltpu
from jax.sharding import PartitionSpec as P


def contract_rows(left, right):
    return lax.dot_general(
        left, right, (((0,), (0,)), ((), ())), preferred_element_type=jnp.float32
    )


def contract_cols(left, right):
    return lax.dot_general(
        left, right, (((1,), (1,)), ((), ())), preferred_element_type=jnp.float32
    )


def swiglu_back(gate, up, dact):
    sig = jax.nn.sigmoid(gate)
    act = (gate * sig * up).astype(jnp.bfloat16)
    dgate = (dact * up * sig * (1.0 + gate * (1.0 - sig))).astype(jnp.bfloat16)
    dup = (dact * gate * sig).astype(jnp.bfloat16)
    return (act, dgate, dup)


def squared(values):
    return jnp.square(values.astype(jnp.float32)).astype(jnp.bfloat16)


def on_device(tokens, out_grad, expert_ids, route_probs, w_gate, w_up, w_down):
    tok_rows = tokens.shape[0]
    width_part = tokens.shape[1]
    top_count = expert_ids.shape[1]
    experts = lax.axis_size("ep")
    capacity = tok_rows * top_count * 9 // (8 * experts)
    assigns = tok_rows * top_count
    flat_ids = expert_ids.reshape(-1)
    onehot = (flat_ids[:, None] == jnp.arange(experts, dtype=jnp.int32)[None, :]).astype(jnp.int32)
    ranks = jnp.sum((jnp.cumsum(onehot, 0) - onehot) * onehot, 1)
    slot_index = flat_ids * capacity + ranks
    table = (
        jnp.full((experts * capacity,), assigns, jnp.int32)
        .at[slot_index]
        .set(jnp.arange(assigns, dtype=jnp.int32))
    )
    token_of = table // top_count
    padded_x = jnp.concatenate([tokens, jnp.zeros((1, width_part), tokens.dtype)], 0)
    padded_dy = jnp.concatenate([out_grad, jnp.zeros((1, width_part), out_grad.dtype)], 0)
    padded_p = jnp.concatenate([route_probs.reshape(-1), jnp.zeros((1,), jnp.float32)], 0)
    send_x = padded_x[token_of].reshape(experts, capacity, width_part)
    send_dy = (padded_dy[token_of].astype(jnp.float32) * padded_p[table][:, None]).astype(
        jnp.bfloat16
    )
    send_dy = send_dy.reshape(experts, capacity, width_part)
    gate_mat = w_gate[0]
    up_mat = w_up[0]
    down_mat = w_down[0]
    recv_x, recv_dy = (
        lax.all_to_all(send_x, "ep", split_axis=0, concat_axis=0, tiled=True),
        lax.all_to_all(send_dy, "ep", split_axis=0, concat_axis=0, tiled=True),
    )
    recv_x = recv_x.reshape(-1, width_part)
    recv_dy = recv_dy.reshape(-1, width_part)
    gate_part = jnp.dot(recv_x, gate_mat, preferred_element_type=jnp.float32)
    up_part = jnp.dot(recv_x, up_mat, preferred_element_type=jnp.float32)
    dact_part = contract_cols(recv_dy, down_mat)
    gate, up, dact = (
        lax.psum(gate_part.astype(jnp.bfloat16), "tp").astype(jnp.float32),
        lax.psum(up_part.astype(jnp.bfloat16), "tp").astype(jnp.float32),
        lax.psum(dact_part.astype(jnp.bfloat16), "tp").astype(jnp.float32),
    )
    act, dgate, dup = swiglu_back(gate, up, dact)
    dx_rows = (contract_cols(dgate, gate_mat) + contract_cols(dup, up_mat)).astype(jnp.bfloat16)
    returned = lax.all_to_all(
        dx_rows.reshape(experts, capacity, width_part),
        "ep",
        split_axis=0,
        concat_axis=0,
        tiled=True,
    )
    scale = 1.0 / tok_rows
    x_sq = squared(recv_x)
    fisher_gate = (contract_rows(x_sq, squared(dgate)) * scale).astype(jnp.bfloat16)[None]
    fisher_up = (contract_rows(x_sq, squared(dup)) * scale).astype(jnp.bfloat16)[None]
    fisher_down = (contract_rows(squared(act), squared(recv_dy)) * scale).astype(jnp.bfloat16)[None]
    pulled = returned.reshape(experts * capacity, width_part)[slot_index].astype(jnp.float32)
    grad_tokens = jnp.sum(pulled.reshape(tok_rows, top_count, width_part), 1).astype(jnp.bfloat16)
    return (grad_tokens, fisher_gate, fisher_up, fisher_down)


MESH = pl.DeviceIdType.MESH
F32 = jnp.float32
BF16 = jnp.bfloat16
ROW_TILE = 16
LANES = 128
VMEM_BYTES = 36 * 1024 * 1024


def flipped(index, mask):
    out, bit = index, 1
    while bit <= mask:
        if mask & bit:
            out = out + bit * (1 - 2 * ((index // bit) % 2))
        bit *= 2
    return out


def slot_rows(tok_rows, top_count, experts):
    capacity = tok_rows * top_count * 9 // (8 * experts)
    return -(-capacity // ROW_TILE) * ROW_TILE


def fused_kernel(
    n_ep, n_tp, rows,
    tok_ref, og_ref, pe_ref, wg_hbm, wu_hbm, wd_hbm,
    grad_ref, fg_hbm, fu_hbm, fd_hbm,
    wg, wu, wd, rank, onehot, peb, tb, sx, rx, pb, rb, sb, rb2, af, dxs, ret, tsq, sqb, fg, fu, fd,
    w_sem, o_sem, pes_sem, per_sem, ts_sem, tr_sem, xs_sem, xr_sem,
    ps_sem, pr_sem, qs_sem, qr_sem, as_sem, ar_sem, ds_sem, dr_sem,
):
    e = lax.axis_index("ep")
    q = lax.axis_index("tp")
    row, mate = e // 2, flipped(e, 1)
    tok_rows, width = tok_ref.shape
    ff = wg.shape[1]
    half = ff // 2
    pair = 2 * rows
    chunks = n_ep // 2
    scale = 1.0 / tok_rows
    blocks = (tok_ref, og_ref)

    loads = [
        pltpu.make_async_copy(hbm.at[0], vmem, w_sem.at[i])
        for i, (hbm, vmem) in enumerate(((wg_hbm, wg), (wu_hbm, wu), (wd_hbm, wd)))
    ]
    for copy in loads:
        copy.start()

    barrier = pltpu.get_barrier_semaphore()
    for k in range(1, n_ep):
        pl.semaphore_signal(barrier, inc=1, device_id=(flipped(e, k), q), device_id_type=MESH)
    for j in range(1, n_tp):
        pl.semaphore_signal(barrier, inc=1, device_id=(e, flipped(q, j)), device_id_type=MESH)
    before = (
        lax.broadcasted_iota(jnp.int32, (tok_rows, tok_rows), 0)
        < lax.broadcasted_iota(jnp.int32, (tok_rows, tok_rows), 1)
    ).astype(BF16)
    slot_iota = lax.broadcasted_iota(jnp.int32, (rows, tok_rows), 0)
    pl.semaphore_wait(barrier, n_ep + n_tp - 2)

    def remote(src, dst, send_sem, recv_sem, device):
        return pltpu.make_async_remote_copy(
            src_ref=src,
            dst_ref=dst,
            send_sem=send_sem,
            recv_sem=recv_sem,
            device_id=device,
            device_id_type=MESH,
        )

    def block(k):
        return pl.ds(k * rows, rows)

    def hop(direction, distance, i):
        step = 1 - 2 * direction
        source = row - step * distance
        src = blocks[i] if distance == 0 else tb.at[source, i]
        return remote(
            src,
            tb.at[source, i],
            ts_sem.at[direction, distance, i],
            tr_sem.at[direction, distance, i],
            (e + 2 * step, q),
        )

    def sends(direction, distance):
        if direction == 0:
            return (row >= distance) & (row < chunks - 1)
        return (row + distance < chunks) & (row > 0)

    def holds(direction, distance):
        if direction == 0:
            return row >= distance
        return row + distance < chunks

    def landed(direction, distance, i):
        source = row - (1 - 2 * direction) * distance
        return remote(
            tb.at[source, i],
            tb.at[source, i],
            ts_sem.at[direction, distance - 1, i],
            tr_sem.at[direction, distance - 1, i],
            (mate, q),
        )

    def arrive(distance, i):
        for direction in range(2):
            if distance:

                @pl.when(holds(direction, distance))
                def _():
                    landed(direction, distance, i).wait_recv()

            if distance < chunks - 1:

                @pl.when(sends(direction, distance))
                def _():
                    hop(direction, distance, i).start()

    pe_copies = [None] * chunks

    def send_probs():
        for c in range(1, chunks):
            pe_copies[c] = remote(
                pe_ref, peb.at[row], pes_sem.at[c], per_sem.at[c], (flipped(e, 2 * c), q)
            )
            pe_copies[c].start()

    def ranked(probs):
        mask = (probs > 0.0).astype(F32)
        ranks = jnp.dot(mask.astype(BF16), before, preferred_element_type=F32)
        rank[...] = jnp.where(mask > 0.0, ranks, -1.0).astype(jnp.int32)

    x_copies = [[None, None] for _ in range(chunks)]

    def select(c, i):
        source = flipped(row, c)
        if c:
            if i == 0:
                pe_copies[c].wait_recv()
            probs, rows_of = peb.at[source], tb.at[source, i]
        else:
            probs, rows_of = pe_ref, blocks[i]
        if i == 0:
            ranked(probs[...])
        for dest, out, k in ((mate, sx, c), (e, rx, 2 * c)):
            hot = (slot_iota == rank[pl.ds(dest, 1), :]).astype(F32)
            picked = jnp.dot(hot.astype(BF16), rows_of[...], preferred_element_type=F32)
            if i:
                picked = picked * jnp.sum(hot * probs[pl.ds(dest, 1), :], 1, keepdims=True)
            out[i, block(k), :] = picked.astype(BF16)
            if out is sx:
                x_copies[c][i] = remote(
                    sx.at[i, block(c), :],
                    rx.at[i, block(2 * c + 1), :],
                    xs_sem.at[c, i],
                    xr_sem.at[c, i],
                    (mate, q),
                )
                x_copies[c][i].start()

    def own_onehot():
        ranked(pe_ref[...])
        for k in range(n_ep):
            onehot[block(k), :] = (slot_iota == rank[pl.ds(flipped(e, k), 1), :]).astype(F32).astype(BF16)

    def piece(index):
        return (
            pl.ds(pl.multiple_of((index // 2) * rows, ROW_TILE), rows),
            pl.ds(pl.multiple_of((index % 2) * half, LANES), half),
        )

    def placed(c, index):
        r = pl.ds(pl.multiple_of(c * pair + (index // 2) * rows, ROW_TILE), rows)
        return af.at[:, r, piece(index)[1]]

    near, far = flipped(q, 1), flipped(q, 2)
    p_copies = [None] * chunks
    q_copies = [None] * chunks
    a_copies = [None] * chunks
    d_copies = [None] * n_ep

    def send_partials(c, first, count):
        for j, other in enumerate((near, flipped(q, 3))):
            r, l = piece(other)
            n = len(p_copies[c])
            copy = remote(
                pb.at[c, pl.ds(first, count), r, l],
                rb.at[c, j, pl.ds(first, count)],
                ps_sem.at[c, n],
                pr_sem.at[c, n],
                (e, near),
            )
            copy.start()
            p_copies[c].append(copy)

    def partials(c):
        p_copies[c] = []
        span = pl.ds(c * pair, pair)
        x_copies[c][0].wait_recv()
        if c == 0:
            for copy in loads:
                copy.wait()
        x = rx[0, span, :]
        pb[c, 0] = jnp.dot(x, wg[...], preferred_element_type=F32).astype(BF16)
        pb[c, 1] = jnp.dot(x, wu[...], preferred_element_type=F32).astype(BF16)
        send_partials(c, 0, 2)
        x_copies[c][1].wait_recv()
        pb[c, 2] = contract_cols(rx[1, span, :], wd[...]).astype(BF16)
        send_partials(c, 2, 1)

    def pair_sum(c):
        r, l = piece(far)
        q_copies[c] = []
        for n, (first, count) in enumerate(((0, 2), (2, 1))):
            p_copies[c][2 * n + 1].wait_recv()
            for i in range(first, first + count):
                sb[c, i] = (pb[c, i, r, l].astype(F32) + rb[c, 1, i].astype(F32)).astype(BF16)
            span = pl.ds(first, count)
            copy = remote(
                sb.at[c, span], rb2.at[c, span], qs_sem.at[c, n], qr_sem.at[c, n], (e, far)
            )
            copy.start()
            q_copies[c].append(copy)

    def activate(c):
        for copy in p_copies[c][0::2] + q_copies[c]:
            copy.wait_recv()
        r, l = piece(q)
        gate, up, dact = [
            pb[c, i, r, l].astype(F32) + rb[c, 0, i].astype(F32) + rb2[c, i].astype(F32)
            for i in range(3)
        ]
        r = pl.ds(pl.multiple_of(c * pair + (q // 2) * rows, ROW_TILE), rows)
        for i, value in enumerate(swiglu_back(gate, up, dact)):
            af[i, r, l] = value
        mine = placed(c, q)
        a_copies[c] = [
            remote(mine, mine, as_sem.at[c, j], ar_sem.at[c, j], (e, other))
            for j, other in enumerate((far, near))
        ]
        for copy in a_copies[c]:
            copy.start()

    def relay(c):
        theirs = placed(c, far)
        remote(theirs, theirs, as_sem.at[c, 0], ar_sem.at[c, 0], (e, far)).wait_recv()
        copy = remote(theirs, theirs, as_sem.at[c, 2], ar_sem.at[c, 2], (e, near))
        copy.start()
        a_copies[c].append(copy)

    def input_grad(c):
        for j, index in ((1, near), (2, flipped(q, 3))):
            theirs = placed(c, index)
            remote(theirs, theirs, as_sem.at[c, j], ar_sem.at[c, j], (e, near)).wait_recv()
        span = pl.ds(c * pair, pair)
        dx = contract_cols(af[1, span, :], wg[...]) + contract_cols(af[2, span, :], wu[...])
        dxs[span, :] = dx.astype(BF16)
        for k in (2 * c, 2 * c + 1):
            if k:
                d_copies[k] = remote(
                    dxs.at[block(k), :],
                    ret.at[block(k), :],
                    ds_sem.at[k],
                    dr_sem.at[k],
                    (flipped(e, k), q),
                )
                d_copies[k].start()
            else:
                ret[block(0), :] = dxs[block(0), :]

    def transposed_squares(source, i, columns):
        @pl.loop(0, columns // LANES)
        def _(step):
            l = pl.ds(pl.multiple_of(step * LANES, LANES), LANES)
            tsq[l, :] = squared(source[i, :, l]).T

    def fisher(columns, depth, out):
        @pl.loop(0, columns // LANES)
        def _(step):
            r = pl.ds(pl.multiple_of(step * LANES, LANES), LANES)
            sums = jnp.dot(tsq[r, :], sqb[:, :depth], preferred_element_type=F32)
            out[r, :] = (sums * scale).astype(BF16)

    stores = []

    def store(i, vmem, hbm):
        copy = pltpu.make_async_copy(vmem, hbm.at[0], o_sem.at[i])
        copy.start()
        stores.append(copy)

    arrive(0, 0)
    send_probs()
    arrive(0, 1)
    for c in range(chunks):
        if c:
            arrive(c, 0)
        select(c, 0)
        if c:
            activate(c - 1)
            arrive(c, 1)
        select(c, 1)
        partials(c)
        if c:
            relay(c - 1)
        pair_sum(c)
        if c:
            input_grad(c - 1)
    last = chunks - 1
    transposed_squares(rx, 0, width)
    activate(last)
    relay(last)
    own_onehot()
    input_grad(last)
    sqb[:, :ff] = squared(af[1])
    fisher(width, ff, fg)
    store(0, fg, fg_hbm)
    sqb[:, :ff] = squared(af[2])
    fisher(width, ff, fu)
    store(1, fu, fu_hbm)
    transposed_squares(af, 0, ff)
    sqb[...] = squared(rx[1])
    fisher(ff, width, fd)
    store(2, fd, fd_hbm)

    for k in range(1, n_ep):
        d_copies[k].wait_recv()
    grad_ref[...] = contract_rows(onehot[...], ret[...]).astype(BF16)

    for distance in range(chunks - 1):
        for direction in range(2):

            @pl.when(sends(direction, distance))
            def _():
                for i in range(2):
                    hop(direction, distance, i).wait_send()

    for copy in pe_copies[1:] + d_copies[1:] + sum(x_copies + p_copies + q_copies + a_copies, []):
        copy.wait_send()
    for copy in stores:
        copy.wait()


def fused_on_device(n_ep, n_tp, tokens, out_grad, expert_ids, route_probs, w_gate, w_up, w_down):
    tok_rows, width = tokens.shape
    ff = w_gate.shape[2]
    rows = slot_rows(tok_rows, expert_ids.shape[1], n_ep)
    total, chunks = n_ep * rows, n_ep // 2
    names = jnp.arange(n_ep, dtype=jnp.int32)[:, None, None]
    probs = jnp.sum(jnp.where(expert_ids[None] == names, route_probs[None], 0.0), 2)
    any_spec = pl.BlockSpec(memory_space=pl.ANY)
    vmem_spec = pl.BlockSpec(memory_space=pltpu.VMEM)
    dma = pltpu.SemaphoreType.DMA
    return pl.pallas_call(
        functools.partial(fused_kernel, n_ep, n_tp, rows),
        out_shape=(
            jax.ShapeDtypeStruct(tokens.shape, BF16),
            jax.ShapeDtypeStruct(w_gate.shape, BF16),
            jax.ShapeDtypeStruct(w_up.shape, BF16),
            jax.ShapeDtypeStruct(w_down.shape, BF16),
        ),
        in_specs=[vmem_spec] * 3 + [any_spec] * 3,
        out_specs=[vmem_spec] + [any_spec] * 3,
        scratch_shapes=[
            pltpu.VMEM((width, ff), BF16),
            pltpu.VMEM((width, ff), BF16),
            pltpu.VMEM((ff, width), BF16),
            pltpu.VMEM((n_ep, tok_rows), jnp.int32),
            pltpu.VMEM((total, tok_rows), BF16),
            pltpu.VMEM((chunks, n_ep, tok_rows), F32),
            pltpu.VMEM((chunks, 2, tok_rows, width), BF16),
            pltpu.VMEM((2, total // 2, width), BF16),
            pltpu.VMEM((2, total, width), BF16),
            pltpu.VMEM((chunks, 3, 2 * rows, ff), BF16),
            pltpu.VMEM((chunks, 2, 3, rows, ff // 2), BF16),
            pltpu.VMEM((chunks, 3, rows, ff // 2), BF16),
            pltpu.VMEM((chunks, 3, rows, ff // 2), BF16),
            pltpu.VMEM((3, total, ff), BF16),
            pltpu.VMEM((total, width), BF16),
            pltpu.VMEM((total, width), BF16),
            pltpu.VMEM((width, total), BF16),
            pltpu.VMEM((total, width), BF16),
            pltpu.VMEM((width, ff), BF16),
            pltpu.VMEM((width, ff), BF16),
            pltpu.VMEM((ff, width), BF16),
            dma((3,)),
            dma((3,)),
            dma((chunks,)),
            dma((chunks,)),
            dma((2, chunks, 2)),
            dma((2, chunks, 2)),
            dma((chunks, 2)),
            dma((chunks, 2)),
            dma((chunks, 4)),
            dma((chunks, 4)),
            dma((chunks, 2)),
            dma((chunks, 2)),
            dma((chunks, 3)),
            dma((chunks, 3)),
            dma((n_ep,)),
            dma((n_ep,)),
        ],
        compiler_params=pltpu.CompilerParams(
            collective_id=0, has_side_effects=True, vmem_limit_bytes=VMEM_BYTES
        ),
    )(tokens, out_grad, probs, w_gate, w_up, w_down)


def part(n_ep, n_tp, *args):
    tokens, expert_ids, w_gate = args[0], args[2], args[4]
    width, ff = w_gate.shape[1:]
    rows = slot_rows(tokens.shape[0], expert_ids.shape[1], n_ep)
    fits = (
        n_tp == 4
        and n_ep in (4, 8)
        and ff <= width
        and ff % (2 * LANES) == 0
        and width % LANES == 0
        and n_ep * rows * (17 * width + 18 * ff) + 14 * width * ff < VMEM_BYTES
    )
    if fits:
        return fused_on_device(n_ep, n_tp, *args)
    return on_device(*args)


def solution(mesh):
    in_specs = (
        P("ep", "tp"),
        P("ep", "tp"),
        P("ep", None),
        P("ep", None),
        P("ep", "tp", None),
        P("ep", "tp", None),
        P("ep", None, "tp"),
    )
    out_specs = (P("ep", "tp"), P("ep", "tp", None), P("ep", "tp", None), P("ep", None, "tp"))
    return jax.shard_map(
        functools.partial(part, mesh.shape["ep"], mesh.shape["tp"]), mesh=mesh, in_specs=in_specs, out_specs=out_specs, check_vma=False
    )
```
